32 devices in a mesh: dp: 8 (over z, x), mp: 4 (over y, core).
Axes of the slice: x: 2, y: 2, z: 4, core: 2. Of those that a mesh axis runs over, the one named last changes fastest.
Arguments:
- images: bfloat16 [64, 196, 768], P('dp'), may hold values from -6 to 6
- group_ids: int32 [64, 1], P('dp'), may hold values from 0 to 15, as said below
- query_gradient: float32 [3072, 768], P('mp', 'dp'), may hold values from -6 to 6
- first_gain: float32 [768], replicated, may hold values from 0.5 to 1.5
- first_bias: float32 [768], replicated, may hold values from -1.5 to 1.5
- token_expand: bfloat16 [196, 384], P(None, 'mp'), may hold values from -0.4375 to 0.4375
- expand_bias: float32 [384], P('mp'), may hold values from -1.5 to 1.5
- token_reduce: bfloat16 [384, 196], P('mp'), may hold values from -0.3125 to 0.3125
- reduce_bias: float32 [196], replicated, may hold values from -1.5 to 1.5
- second_gain: float32 [768], replicated, may hold values from 0.5 to 1.5
- second_bias: float32 [768], replicated, may hold values from -1.5 to 1.5
- channel_expand: bfloat16 [768, 3072], P(None, 'mp'), may hold values from -0.21875 to 0.21875
- channel_bias: float32 [3072], P('mp'), may hold values from -1.5 to 1.5
- channel_reduce: bfloat16 [3072, 768], P('mp'), may hold values from -0.109375 to 0.109375
- output_bias: float32 [768], replicated, may hold values from -1.5 to 1.5
- cotangent: bfloat16 [64, 196, 768], P('dp'), may hold values from -5.6 to 5.6
Outputs:
- block_output: bfloat16 [64, 196, 768], P('dp')
- input_grad: float32 [64, 196, 768], P('dp')
- first_gain_gradient: float32 [768], replicated
- first_bias_gradient: float32 [768], replicated
- token_expand_gradient: float32 [196, 384], P(None, 'mp')
- expand_bias_gradient: float32 [384], P('mp')
- token_reduce_gradient: float32 [384, 196], P('mp')
- reduce_bias_gradient: float32 [196], replicated
- second_gain_gradient: float32 [768], replicated
- second_bias_gradient: float32 [768], replicated
- channel_expand_gradient: float32 [768, 3072], P(None, 'mp')
- channel_bias_gradient: float32 [3072], P('mp')
- channel_reduce_gradient: float32 [3072, 768], P('mp', 'dp')
- output_bias_gradient: float32 [768], replicated
- group_norms: float32 [16], replicated
- influence: float32 [16], replicated
The draws below stay inside these ranges and needn't reach their ends.
Inputs may be any that keep to these rules, and one draw needn't show every extreme that they name: `group_ids`: every one of the 16 groups marks at least one image.
All inputs are finite; a program needn't handle non-finite values.
Results may differ from the reference program's by a relative error of at most 0.02.
Values may be sent and summed in bfloat16 or wider, within the bound.
No kernel may reach another device: no remote copies, remote signals or barrier semaphores. Data moves between devices by JAX's collectives and lax.ppermute only.
A program may use at most 192 MiB of HBM per device.

```python
import jax
import jax.numpy as jnp
import numpy as np
from jax import lax

D = 768
DC = 3072
S = 196
DS = 384
GROUPS = 16
IMAGES = 64


def group_labels(key):
    base_key = jax.random.fold_in(key, 7)
    cumulative = np.cumsum(np.array([1680 // (position + 1) for position in range(GROUPS)], dtype=np.int64))
    uniform_draws = jax.random.randint(jax.random.fold_in(base_key, 1), (IMAGES,), 0, int(cumulative[-1]), dtype=jnp.int32)
    bounds = jnp.asarray(cumulative[:-1].astype(np.int32))
    popularity = jnp.sum((uniform_draws[:, None] >= bounds[None, :]).astype(jnp.int32), axis=1)
    group_order = jax.random.permutation(jax.random.fold_in(base_key, 2), GROUPS).astype(jnp.int32)
    labels = jnp.take(group_order, popularity)
    anchor_rows = jax.random.permutation(jax.random.fold_in(base_key, 3), IMAGES)[:GROUPS]
    labels = labels.at[anchor_rows].set(jnp.arange(GROUPS, dtype=jnp.int32))
    return labels.astype(jnp.int32)


def draw_group_ids(key, part):
    return group_labels(key)[:, None]


def draw_cotangent(key, part):
    labels = group_labels(key)
    pattern_key = jax.random.fold_in(key, 11)
    noise_key = jax.random.fold_in(key, 12)
    noise = jnp.clip(jax.random.normal(noise_key, (IMAGES, S, D), jnp.float32), -4.0, 4.0) * 0.6
    pattern = jnp.clip(jax.random.normal(pattern_key, (GROUPS, S, D), jnp.float32), -4.0, 4.0) * 0.8
    values = noise + jnp.take(pattern, labels, axis=0)
    return values.astype(jnp.bfloat16)


def block_levels(own_key, dims, shards, low, largest):
    def one(dim, parts):
        steps = jax.random.uniform(jax.random.fold_in(jax.random.fold_in(own_key, 6), dim), (parts,), jnp.float32, low / len(shards), largest / len(shards))
        return jnp.repeat(jnp.exp(steps), dims[dim] // parts).reshape((-1,) + (1,) * (len(dims) - dim - 1))

    gain = one(*shards[0])
    for cut in shards[1:]:
        gain = gain * one(*cut)
    return gain


def centred(key, extent, spread, reach, split=(), held_as=jnp.bfloat16):
    entries = spread * jax.random.normal(key, extent, jnp.float32)
    if split:
        entries = entries * block_levels(key, extent, split, -0.22, 0.18)
    return jnp.clip(entries, -reach, reach).astype(held_as)


def setup_inputs(seed: int = 0) -> dict:
    key_of = jax.random.split(jax.random.key(seed), 17)
    return {
        "images": centred(key_of[0], (IMAGES, S, D), 1.0, 6.0, ((0, 8),)),
        "group_ids": draw_group_ids(jax.random.fold_in(key_of[16], 71), 0),
        "query_gradient": centred(key_of[2], (DC, D), 1.0, 6.0, ((0, 4), (1, 8)), jnp.float32),
        "first_gain": jnp.clip(1.0 + 0.1 * jax.random.normal(key_of[3], (D,), jnp.float32), 0.5, 1.5),
        "first_bias": centred(key_of[4], (D,), 0.3, 1.5, (), jnp.float32),
        "token_expand": centred(key_of[5], (S, DS), S ** -0.5, 0.4375, ((1, 4),)),
        "expand_bias": centred(key_of[6], (DS,), 0.3, 1.5, ((0, 4),), jnp.float32),
        "token_reduce": centred(key_of[7], (DS, S), DS ** -0.5, 0.3125, ((0, 4),)),
        "reduce_bias": centred(key_of[8], (S,), 0.3, 1.5, (), jnp.float32),
        "second_gain": jnp.clip(1.0 + 0.1 * jax.random.normal(key_of[9], (D,), jnp.float32), 0.5, 1.5),
        "second_bias": centred(key_of[10], (D,), 0.3, 1.5, (), jnp.float32),
        "channel_expand": centred(key_of[11], (D, DC), D ** -0.5, 0.21875, ((1, 4),)),
        "channel_bias": centred(key_of[12], (DC,), 0.3, 1.5, ((0, 4),), jnp.float32),
        "channel_reduce": centred(key_of[13], (DC, D), DC ** -0.5, 0.109375, ((0, 4),)),
        "output_bias": centred(key_of[14], (D,), 0.3, 1.5, (), jnp.float32),
        "cotangent": draw_cotangent(jax.random.fold_in(key_of[16], 71), 0),
    }


@jax.custom_vjp
def low(v):
    return lax.optimization_barrier(v.astype(jnp.bfloat16)).astype(jnp.float32)

@jax.custom_vjp
def low_back(v):
    return v

def low_keep(v):
    return (low(v), None)

def low_pass(kept, grad):
    return (grad,)

def back_keep(v):
    return (v, None)

def back_low(kept, grad):
    return (low(grad),)
low.defvjp(low_keep, low_pass)
low_back.defvjp(back_keep, back_low)
epsilon = 1e-06
highest = lax.Precision.HIGHEST

def layer_norm(inputs, norm_gain, norm_bias):
    center = inputs - lax.optimization_barrier(jnp.mean(inputs, axis=-1, keepdims=True))
    scaled = center * lax.rsqrt(lax.optimization_barrier(jnp.mean(center * center, axis=-1, keepdims=True)) + epsilon)
    return scaled * norm_gain + norm_bias

def gelu_tanh(inputs):
    return jax.nn.gelu(inputs, approximate=True)

def forward(params, image_rows, group_shift, member_ids):
    first_gain, first_bias, token_expand, expand_bias, token_reduce, reduce_bias, second_gain, second_bias, channel_expand, channel_bias, channel_reduce, output_bias = params
    normed = low(layer_norm(image_rows, first_gain, first_bias))
    token_pre = low_back(jnp.einsum('bsd,sh->bhd', normed, token_expand, precision=highest) + expand_bias[:, None])
    token_act = low(gelu_tanh(token_pre))
    token_mix = low_back(jnp.einsum('bhd,hs->bsd', token_act, token_reduce, precision=highest) + reduce_bias[:, None])
    middle = image_rows + token_mix
    second = low(layer_norm(middle, second_gain, second_bias))
    channel_pre = low_back(jnp.einsum('bsd,df->bsf', second, channel_expand, precision=highest) + channel_bias)
    channel_act = low(gelu_tanh(channel_pre))
    weights = channel_reduce[None] + jnp.take(group_shift, member_ids, axis=0)
    channel_mix = low_back(jnp.einsum('bsf,bfd->bsd', channel_act, weights, precision=highest) + output_bias)
    return middle + channel_mix

def reference(images, group_ids, query_gradient, first_gain, first_bias, token_expand, expand_bias, token_reduce, reduce_bias, second_gain, second_bias, channel_expand, channel_bias, channel_reduce, output_bias, cotangent):
    params = jax.tree.map(lambda entry: entry.astype(jnp.float32), (first_gain, first_bias, token_expand, expand_bias, token_reduce, reduce_bias, second_gain, second_bias, channel_expand, channel_bias, channel_reduce, output_bias))
    count = images.shape[0]
    batches = count // 8
    stacked = images.reshape(batches, 8, S, D)
    labels = group_ids[:, 0].astype(jnp.int32).reshape(batches, 8)
    cot_stacked = cotangent.reshape(batches, 8, S, D)
    zero_shift = jnp.zeros((GROUPS, DC, D), jnp.float32)

    def visit(carry, inputs):
        totals, shift_total = carry
        image_rows, member_ids, cot_rows = inputs

        def local(param_set, rows, shift):
            return forward(param_set, rows, shift, member_ids)
        result, pullback = jax.vjp(local, params, image_rows.astype(jnp.float32), zero_shift)
        param_grads, row_grads, shift_grads = pullback(cot_rows.astype(jnp.float32))
        totals = jax.tree.map(jnp.add, totals, param_grads)
        return ((totals, shift_total + shift_grads), (result.astype(jnp.bfloat16), row_grads))
    start = (jax.tree.map(jnp.zeros_like, params), zero_shift)
    (totals, group_grad), (outputs, input_rows) = lax.scan(visit, start, (stacked, labels, cot_stacked))
    block_output = outputs.reshape(count, S, D)
    input_grad = input_rows.reshape(count, S, D)
    norm_raw = jnp.sqrt(lax.optimization_barrier(jnp.sum(group_grad * group_grad, axis=(1, 2))))
    average = jnp.mean(norm_raw)
    factor = average / jnp.maximum(norm_raw, average)
    products = lax.optimization_barrier(jnp.sum(group_grad * query_gradient.astype(jnp.float32), axis=(1, 2)))
    influence = factor * products / average
    group_norms = norm_raw / average
    return (block_output, input_grad, totals[0], totals[1], totals[2], totals[3], totals[4], totals[5], totals[6], totals[7], totals[8], totals[9], totals[10], totals[11], group_norms, influence)
```

```python
import functools

import jax
import jax.numpy as jnp
from jax import lax
from jax.experimental import pallas as pl
from jax.experimental.pallas import tpu as pltpu
from jax.sharding import PartitionSpec as P

GROUPS = 16
EPS = 1e-06
BF = jnp.bfloat16
F32 = jnp.float32
CORES = 2
PAD = 4
TR = 256
EB = 512
PACK = 640
ROOT = 0.7978845608028654
CUBE = 0.044715


def dot(a, b, ca, cb):
    return lax.dot_general(a, b, (((ca,), (cb,)), ((), ())), preferred_element_type=F32)


def normal(v):
    center = v - jnp.mean(v, axis=-1, keepdims=True)
    inverse = lax.rsqrt(jnp.mean(center * center, axis=-1, keepdims=True) + EPS)
    return center * inverse, inverse


def normal_back(scaled, unit, inverse):
    return inverse * (
        scaled
        - jnp.mean(scaled, axis=-1, keepdims=True)
        - unit * jnp.mean(scaled * unit, axis=-1, keepdims=True)
    )


def gelu(v):
    t = jnp.tanh(v * (ROOT + ROOT * CUBE * (v * v)))
    return (0.5 * v) * (1.0 + t)


def gelu_both(v):
    square = v * v
    t = jnp.tanh(v * (ROOT + ROOT * CUBE * square))
    half = 0.5 * v
    rise = 0.5 + 0.5 * t
    slope = rise + half * (1.0 - t * t) * (ROOT + 3.0 * ROOT * CUBE * square)
    return v * rise, slope


def column(row):
    n = row.shape[-1]
    eye = lax.broadcasted_iota(jnp.int32, (n, n), 0) == lax.broadcasted_iota(jnp.int32, (n, n), 1)
    return jnp.sum(jnp.where(eye, row, 0.0), axis=1, keepdims=True)


def flat(col):
    n = col.shape[0]
    eye = lax.broadcasted_iota(jnp.int32, (n, n), 0) == lax.broadcasted_iota(jnp.int32, (n, n), 1)
    return jnp.sum(jnp.where(eye, col, 0.0), axis=0, keepdims=True)


def tokens_in_order(place, packs, te, tr, eb, patches):
    row, core = place[1], place[0]
    for k, pack in enumerate(packs):
        count, rows = pack.shape[0], pack.shape[1]
        for u in range(count):
            at = pl.multiple_of(((row ^ u) * CORES + (core ^ k)) * rows, 16)
            te[pl.ds(at, rows), :] = pack[u, :, 0:patches]
            tr[pl.ds(at, rows), :] = pack[u, :, TR : TR + patches]
            eb[pl.ds(at, rows), :] = pack[u, :, EB : EB + 1].astype(F32)


def forward_kernel(g, place, *refs):
    (pack_own, pack_other, image, cot, params, reduce_bias) = refs[:6]
    expand = refs[6:8]
    reduce = refs[8:10]
    bias = refs[10:12]
    acts = refs[12 : 12 + g.Z]
    part, middle, low_out, grad_own, grad_other = refs[12 + g.Z : 17 + g.Z]
    te, tr, eb, rb, held = refs[17 + g.Z :]

    @pl.when(pl.program_id(0) == 0)
    def _():
        tokens_in_order(place, (pack_own, pack_other), te, tr, eb, g.S)
        rb[...] = column(reduce_bias[...])

    pixels = image[0].astype(F32)
    unit, _ = normal(pixels)
    low = (unit * params[0:1] + params[1:2]).astype(BF)
    token = gelu(dot(te[...], low, 1, 0) + eb[...]).astype(BF)
    mid = pixels + dot(tr[...], token, 0, 0) + rb[...]
    middle[0] = mid
    unit, _ = normal(mid)
    low = (unit * params[2:3] + params[3:4]).astype(BF)
    low_out[0] = low
    total = None
    for r in range(CORES):
        act, slope = gelu_both(dot(low, expand[r][...], 1, 0) + bias[r][...])
        act = act.astype(BF)
        for h in range(g.Z // 2):
            held[r * (g.Z // 2) + h] = act[:, h * g.FC : (h + 1) * g.FC]
        hidden = dot(cot[0], reduce[r][...], 1, 1)
        grad = (slope * hidden).astype(BF)
        (grad_own, grad_other)[r][0] = grad
        term = dot(grad, expand[r][...], 1, 1)
        total = term if total is None else total + term
    part[0] = total.astype(BF)
    core, depth = place[0], place[2]
    for s in range(g.Z):
        owner = depth ^ s
        r = (owner // (g.Z // 2)) ^ core
        acts[s][0] = held[r * (g.Z // 2) + owner % (g.Z // 2)]


def mix_kernel(g, place, *refs):
    acts = refs[: g.Z]
    low, grad_own, grad_other, cot = refs[g.Z : g.Z + 4]
    reduce = refs[g.Z + 4 : g.Z + 6]
    mixed, own, other, sums = refs[g.Z + 6 : g.Z + 10]
    keep, give, rows, held = refs[g.Z + 10 :]
    first = pl.program_id(0) == 0
    last = pl.program_id(0) == pl.num_programs(0) - 1
    core, depth = place[0], place[2]
    for s in range(g.Z):
        owner = depth ^ s
        r = (owner // (g.Z // 2)) ^ core
        held[r * (g.Z // 2) + owner % (g.Z // 2)] = acts[s][0]
    total = None
    for r in range(CORES):
        for h in range(g.Z // 2):
            term = dot(
                held[r * (g.Z // 2) + h], reduce[r][h * g.FC : (h + 1) * g.FC, :], 1, 0
            )
            total = term if total is None else total + term
    mixed[0] = total.astype(BF)

    @pl.when(first)
    def _():
        keep[...] = jnp.zeros_like(keep)
        give[...] = jnp.zeros_like(give)
        rows[...] = jnp.zeros_like(rows)

    keep[...] += dot(low[0], grad_own[0], 0, 0)
    give[...] += dot(low[0], grad_other[0], 0, 0)
    rows[0:1, : g.D] += jnp.sum(cot[0].astype(F32), axis=0, keepdims=True)
    mine = jnp.sum(grad_own[0].astype(F32), axis=0, keepdims=True)
    theirs = jnp.sum(grad_other[0].astype(F32), axis=0, keepdims=True)
    rows[1:2, : g.FS] += jnp.where(core == 0, mine, theirs)
    rows[2:3, : g.FS] += jnp.where(core == 0, theirs, mine)

    @pl.when(last)
    def _():
        own[...] = keep[...]
        other[...] = give[...].astype(BF)
        sums[...] = rows[...]


def backward_kernel(g, place, *refs):
    (pack_own, pack_other, image, cot, middle, params, sums) = refs[:7]
    parts = refs[7 : 7 + g.Y]
    grad_out, mine, theirs = refs[7 + g.Y : 10 + g.Y]
    te, tr, eb, act, pre_grad, tr_grad, te_grad, eb_grad, rb_grad, rows = refs[10 + g.Y :]
    first = pl.program_id(0) == 0
    last = pl.program_id(0) == pl.num_programs(0) - 1
    core, row = place[0], place[1]

    @pl.when(first)
    def _():
        tokens_in_order(place, (pack_own, pack_other), te, tr, eb, g.S)
        tr_grad[...] = jnp.zeros_like(tr_grad)
        te_grad[...] = jnp.zeros_like(te_grad)
        eb_grad[...] = jnp.zeros_like(eb_grad)
        rb_grad[...] = jnp.zeros_like(rb_grad)
        rows[...] = jnp.zeros_like(rows)

    second = tree([p[0].astype(F32) for p in parts])
    unit, inverse = normal(middle[0])
    mid_grad = cot[0].astype(F32) + normal_back(second * params[2:3], unit, inverse)
    low_grad = mid_grad.astype(BF)
    rows[2:3] += jnp.sum(second * unit, axis=0, keepdims=True)
    rows[3:4] += jnp.sum(second, axis=0, keepdims=True)
    rb_grad[...] += jnp.sum(low_grad.astype(F32), axis=1, keepdims=True)

    unit, inverse = normal(image[0].astype(F32))
    low = (unit * params[0:1] + params[1:2]).astype(BF)
    value, slope = gelu_both(dot(te[...], low, 1, 0) + eb[...])
    act[...] = value.astype(BF)
    token_grad = (slope * dot(tr[...], low_grad, 1, 0)).astype(BF)
    pre_grad[...] = token_grad
    eb_grad[...] += jnp.sum(token_grad.astype(F32), axis=1, keepdims=True)
    plane = CORES * g.HS
    at = pl.ds(pl.multiple_of(row * plane, 16), plane)
    tr_grad[...] += dot(act[at, :], low_grad, 1, 1)
    te_grad[...] += dot(pre_grad[at, :], low, 1, 1)
    first_grad = dot(te[...], token_grad, 0, 0)
    rows[0:1] += jnp.sum(first_grad * unit, axis=0, keepdims=True)
    rows[1:2] += jnp.sum(first_grad, axis=0, keepdims=True)
    grad_out[0] = mid_grad + normal_back(first_grad * params[0:1], unit, inverse)

    @pl.when(last)
    def _():
        rows[4:5, : g.S] = flat(rb_grad[...])
        rows[5:8] = sums[0:3]
        for k, out in ((0, mine), (1, theirs)):
            out[...] = jnp.zeros_like(out)
            shard = core ^ k
            at = pl.ds(pl.multiple_of(shard * g.HS, 16), g.HS)
            out[0 : g.HS, 0 : g.S] = te_grad[at, :].astype(BF)
            out[0 : g.HS, TR : TR + g.S] = tr_grad[at, :].astype(BF)
            at = pl.ds(pl.multiple_of((row * CORES + shard) * g.HS, 16), g.HS)
            out[0 : g.HS, EB : EB + 1] = eb_grad[at, :].astype(BF)
            out[g.HS : g.HS + 16, :] = rows[...].astype(BF)


def tree(terms):
    while len(terms) > 1:
        terms = [terms[k] + terms[k + 1] for k in range(0, len(terms), 2)]
    return terms[0]


def small_kernel(g, place, *refs):
    pieces = refs[: g.Z]
    outs = refs[g.Z :]
    total = tree([p[...].astype(F32) for p in pieces])
    (first_gain, first_bias, te, eb, tr, rb, second_gain, second_bias, bias, out_bias) = outs
    te[...] = total[0 : g.HS, 0:256].T[0 : g.S, :]
    tr[...] = total[0 : g.HS, TR : TR + g.S]
    eb[...] = flat(total[0 : g.HS, EB : EB + 1])
    base = g.HS
    first_gain[...] = total[base : base + 1]
    first_bias[...] = total[base + 1 : base + 2]
    second_gain[...] = total[base + 2 : base + 3]
    second_bias[...] = total[base + 3 : base + 4]
    rb[...] = total[base + 4 : base + 5, : g.S]
    out_bias[...] = total[base + 5 : base + 6]
    bias[...] = jnp.where(
        place[0] == 0, total[base + 6 : base + 7, : g.FS], total[base + 7 : base + 8, : g.FS]
    )


def output_kernel(g, place, middle, params, *refs):
    parts, out = refs[: g.Y], refs[g.Y]
    mixed = tree([p[0].astype(F32) for p in parts])
    out[0] = (middle[0] + mixed + params[4:5]).astype(BF)


def join_kernel(place, own, other, out):
    k = pl.program_id(0)

    @pl.when(k == 0)
    def _():
        out[...] = own[...]

    @pl.when(k == 1)
    def _():
        out[...] = other[...]


def group_kernel(g, place, *refs):
    acts = refs[: g.Z * g.X]
    near = refs[g.Z * g.X : g.Z * g.X + g.X]
    far = refs[g.Z * g.X + g.X : g.Z * g.X + g.X + (g.Z - 1) * g.Y]
    own, give, act_held, cot_held, total, act_sems, cot_sems = refs[-7:]
    core, row = place[0], place[1]
    act_copies, cot_copies = {}, {}
    for s in range(g.Z):
        for t in range(g.X):
            k = s * g.X + t
            act_copies[s, t] = pltpu.make_async_copy(acts[k], act_held.at[k], act_sems.at[k])
            act_copies[s, t].start()
        if s == 0:
            for t in range(g.X):
                copy = pltpu.make_async_copy(near[t], cot_held.at[t], cot_sems.at[t])
                copy.start()
                cot_copies.setdefault(s, []).append(copy)
        else:
            for u in range(g.Y):
                at = pl.ds((row ^ u) * g.IY, g.IY)
                n = g.X + (s - 1) * g.Y + u
                copy = pltpu.make_async_copy(
                    far[(s - 1) * g.Y + u],
                    cot_held.at[pl.ds(s * g.X, g.X), at],
                    cot_sems.at[n],
                )
                copy.start()
                cot_copies.setdefault(s, []).append(copy)
    total[...] = jnp.zeros_like(total)
    for s in range(g.Z):
        for t in range(g.X):
            act_copies[s, t].wait()
        for copy in cot_copies[s]:
            copy.wait()

        @pl.loop(0, g.X * g.IB)
        def _(n):
            k, j = s * g.X + n // g.IB, n % g.IB
            tail = cot_held[k, j, g.S - 4 : g.S + PAD, 0:128].astype(F32)
            rows = lax.broadcasted_iota(jnp.int32, tail.shape, 0)
            group = jnp.max(jnp.where(rows >= 4, tail, 0.0)).astype(jnp.int32)
            total[group] += dot(act_held[k, j], cot_held[k, j, 0 : g.S, :], 0, 0)

    half = g.FC // 2
    at = pl.ds(pl.multiple_of(core * half, 8), half)
    off = pl.ds(pl.multiple_of((1 - core) * half, 8), half)
    for k in range(GROUPS):
        own[k] = total[k, at, :]
        give[k] = total[k, off, :].astype(BF)


def score_kernel(g, place, own, other, query, total, scores, held):
    k = pl.program_id(0)
    slot = place[3]

    @pl.when(k == 0)
    def _():
        held[...] = jnp.concatenate([query[slot ^ n] for n in range(g.Z)], axis=1)
        scores[...] = jnp.zeros_like(scores)
        total[...] = jnp.zeros_like(total)

    grad = own[0] + other[0].astype(F32)
    square = jnp.sum(jnp.sum(grad * grad, axis=0, keepdims=True), axis=1, keepdims=True)
    product = jnp.sum(jnp.sum(grad * held[...], axis=0, keepdims=True), axis=1, keepdims=True)
    rows = lax.broadcasted_iota(jnp.int32, scores.shape, 0)
    lanes = lax.broadcasted_iota(jnp.int32, scores.shape, 1)
    here = lanes == k
    scores[...] += jnp.where(here & (rows == 0), square, 0.0) + jnp.where(
        here & (rows == 1), product, 0.0
    )
    for n in range(g.Z):
        total[n] += grad[:, n * g.DC : (n + 1) * g.DC]


class Geometry:
    def __init__(self, dp, mp, images, token_reduce, channel_expand):
        self.X = 1 << ((dp.bit_length() - 1) // 2)
        self.Z = dp // self.X
        self.Y = mp // CORES
        self.MP = mp
        self.B, self.S, self.D = images.shape
        self.IB = self.B // CORES
        self.IY = self.IB // self.Y
        self.HS = token_reduce.shape[0]
        self.FS = channel_expand.shape[1]
        self.FC = self.FS * CORES // self.Z
        self.DX = self.D // self.X
        self.DC = self.D // dp

    def x(self, t):
        return [
            (z * self.X + x, z * self.X + (x ^ t)) for z in range(self.Z) for x in range(self.X)
        ]

    def z(self, s):
        return [
            (z * self.X + x, (z ^ s) * self.X + x) for z in range(self.Z) for x in range(self.X)
        ]

    def y(self, u):
        return [
            (y * CORES + c, (y ^ u) * CORES + c) for y in range(self.Y) for c in range(CORES)
        ]

    def core(self):
        return [(m, m ^ 1) for m in range(self.MP)]

    def owners(self, r):
        pairs = []
        for p in range(self.Z * self.X):
            for m in range(self.MP):
                y, c = divmod(m, CORES)
                x, k = divmod(p, self.Z)
                j = k ^ r
                z = c * (self.Z // 2) + j // 2
                pairs.append((p * self.MP + m, (z * self.X + x) * self.MP + y * CORES + j % 2))
        return pairs


def whole(shape):
    return pl.BlockSpec(shape, lambda i, place: (0,) * len(shape))


def call(kernel, name, place, grid, args, in_specs, out_shape, out_specs, scratch, flops, nbytes):
    return pl.pallas_call(
        kernel,
        name=name,
        grid_spec=pltpu.PrefetchScalarGridSpec(
            num_scalar_prefetch=1,
            grid=grid,
            in_specs=in_specs,
            out_specs=out_specs,
            scratch_shapes=scratch,
        ),
        out_shape=out_shape,
        compiler_params=pltpu.CompilerParams(vmem_limit_bytes=56 << 20),
        cost_estimate=pl.CostEstimate(flops=flops, bytes_accessed=nbytes, transcendentals=0),
    )(place, *args)


def shape(dims, dtype):
    return jax.ShapeDtypeStruct(tuple(dims), dtype)


def select(pieces, index):
    out = pieces[0]
    for k in range(1, len(pieces)):
        out = jnp.where(index == k, pieces[k], out)
    return out


def per_device(
    images,
    group_ids,
    query_gradient,
    first_gain,
    first_bias,
    token_expand,
    expand_bias,
    token_reduce,
    reduce_bias,
    second_gain,
    second_bias,
    channel_expand,
    channel_bias,
    channel_reduce,
    output_bias,
    cotangent,
):
    g = Geometry(
        lax.axis_size("dp"), lax.axis_size("mp"), images, token_reduce, channel_expand
    )
    p, m = lax.axis_index("dp"), lax.axis_index("mp")
    depth, x = p // g.X, p % g.X
    row, core = m // CORES, m % CORES
    slot = (depth % (g.Z // 2)) * 2 + core
    place = jnp.stack([core, row, depth, slot]).astype(jnp.int32)
    S, D, IB = g.S, g.D, g.IB
    both = ("dp", "mp")

    pack = jnp.concatenate(
        [
            jnp.pad(token_expand.T, ((0, 0), (0, TR - S))),
            jnp.pad(token_reduce, ((0, 0), (0, EB - TR - S))),
            jnp.pad(expand_bias.astype(BF)[:, None], ((0, 0), (0, PACK - EB - 1))),
        ],
        axis=1,
    )
    packs = jnp.stack([pack] + [lax.ppermute(pack, "mp", g.y(u)) for u in range(1, g.Y)])
    packs_other = lax.ppermute(packs, "mp", g.core())
    expand_other = lax.ppermute(channel_expand, "mp", g.core())
    reduce_other = lax.ppermute(channel_reduce, "mp", g.core())
    bias_own = channel_bias[None]
    bias_other = lax.ppermute(bias_own, "mp", g.core())
    params = jnp.concatenate(
        [
            jnp.stack([first_gain, first_bias, second_gain, second_bias, output_bias]),
            jnp.zeros((3, D), F32),
        ]
    )

    labels = jnp.broadcast_to(group_ids.astype(BF)[:, :, None], (g.B, PAD, g.DX))

    def columns(target):
        piece = select([cotangent[:, :, k * g.DX : (k + 1) * g.DX] for k in range(g.X)], target)
        piece = jnp.concatenate([piece, labels], axis=1)
        return lax.dynamic_slice_in_dim(piece, core * IB, IB, 0)

    near = [columns(x)] + [
        lax.ppermute(columns(x ^ t), "dp", g.x(t)) for t in range(1, g.X)
    ]
    block = jnp.stack([lax.dynamic_slice_in_dim(v, row * g.IY, g.IY, 0) for v in near])
    blocks = {0: block}
    for s in range(1, g.Z):
        bit = s & -s
        blocks[s] = lax.ppermute(blocks[s ^ bit], "dp", g.z(bit))
    far = []
    for s in range(1, g.Z):
        far.append(blocks[s])
        for u in range(1, g.Y):
            far.append(lax.ppermute(blocks[s], "mp", g.y(u)))

    query_rows = query_gradient.reshape(g.Z, g.FC // 2, g.DC)
    query = jnp.stack(
        [
            lax.ppermute(
                lax.dynamic_index_in_dim(query_rows, (p % g.Z) ^ r, 0, False), both, g.owners(r)
            )
            for r in range(g.Z)
        ]
    )

    image_spec = pl.BlockSpec((1, S, D), lambda i, place: (place[0] * IB + i, 0, 0))
    row_spec = pl.BlockSpec((1, S, D), lambda i, place: (i, 0, 0))
    hidden_spec = pl.BlockSpec((1, S, g.FS), lambda i, place: (i, 0, 0))
    chunk_spec = pl.BlockSpec((1, S, g.FC), lambda i, place: (i, 0, 0))
    pack_spec = whole((g.Y, g.HS, PACK))
    units = g.HS * g.MP
    token_scratch = [
        pltpu.VMEM((units, S), BF),
        pltpu.VMEM((units, S), BF),
        pltpu.VMEM((units, 1), F32),
    ]
    matmul = 2 * IB * S * D * g.FS * CORES
    outs = call(
        functools.partial(forward_kernel, g),
        "forward",
        place,
        (IB,),
        (
            packs,
            packs_other,
            images,
            cotangent,
            params,
            reduce_bias[None],
            channel_expand,
            expand_other,
            channel_reduce,
            reduce_other,
            bias_own,
            bias_other,
        ),
        [
            pack_spec,
            pack_spec,
            image_spec,
            image_spec,
            whole((8, D)),
            whole((1, S)),
            whole((D, g.FS)),
            whole((D, g.FS)),
            whole((g.FS, D)),
            whole((g.FS, D)),
            whole((1, g.FS)),
            whole((1, g.FS)),
        ],
        [shape((IB, S, g.FC), BF)] * g.Z
        + [
            shape((IB, S, D), BF),
            shape((IB, S, D), F32),
            shape((IB, S, D), BF),
            shape((IB, S, g.FS), BF),
            shape((IB, S, g.FS), BF),
        ],
        [chunk_spec] * g.Z + [row_spec, row_spec, row_spec, hidden_spec, hidden_spec],
        token_scratch + [pltpu.VMEM((S, 1), F32), pltpu.VMEM((g.Z, S, g.FC), BF)],
        3 * matmul,
        20 << 20,
    )
    acts = outs[: g.Z]
    part, middle, low, grad_own, grad_other = outs[g.Z :]
    parts = [part] + [lax.ppermute(part, "mp", g.y(u)) for u in range(1, g.Y)]

    act_grid = {}
    for s in range(g.Z):
        act_grid[s, 0] = acts[s] if s == 0 else lax.ppermute(acts[s], "dp", g.z(s))
        for t in range(1, g.X):
            act_grid[s, t] = lax.ppermute(act_grid[s, 0], "dp", g.x(t))

    mixed, keep, give, sums = call(
        functools.partial(mix_kernel, g),
        "mix",
        place,
        (IB,),
        (*acts, low, grad_own, grad_other, cotangent, channel_reduce, reduce_other),
        [chunk_spec] * g.Z
        + [row_spec, hidden_spec, hidden_spec, image_spec, whole((g.FS, D)), whole((g.FS, D))],
        [
            shape((IB, S, D), BF),
            shape((D, g.FS), F32),
            shape((D, g.FS), BF),
            shape((8, D), F32),
        ],
        [row_spec, whole((D, g.FS)), whole((D, g.FS)), whole((8, D))],
        [
            pltpu.VMEM((D, g.FS), F32),
            pltpu.VMEM((D, g.FS), F32),
            pltpu.VMEM((8, D), F32),
            pltpu.VMEM((g.Z, S, g.FC), BF),
        ],
        2 * matmul,
        16 << 20,
    )
    mixes = [mixed] + [lax.ppermute(mixed, "mp", g.y(u)) for u in range(1, g.Y)]
    expand_part = keep + lax.ppermute(give, "mp", g.core()).astype(F32)
    channel_expand_gradient = lax.psum(expand_part.astype(BF), "dp").astype(F32)

    plane = CORES * g.HS
    grad_own_rows, mine, theirs = call(
        functools.partial(backward_kernel, g),
        "backward",
        place,
        (IB,),
        (packs, packs_other, images, cotangent, middle, params, sums, *parts),
        [
            pack_spec,
            pack_spec,
            image_spec,
            image_spec,
            row_spec,
            whole((8, D)),
            whole((8, D)),
        ]
        + [row_spec] * g.Y,
        [shape((IB, S, D), F32), shape((g.HS + 16, D), BF), shape((g.HS + 16, D), BF)],
        [row_spec, whole((g.HS + 16, D)), whole((g.HS + 16, D))],
        token_scratch
        + [
            pltpu.VMEM((units, D), BF),
            pltpu.VMEM((units, D), BF),
            pltpu.VMEM((plane, S), F32),
            pltpu.VMEM((plane, S), F32),
            pltpu.VMEM((units, 1), F32),
            pltpu.VMEM((S, 1), F32),
            pltpu.VMEM((16, D), F32),
        ],
        8 * IB * S * D * units,
        16 << 20,
    )

    def joined(own, name):
        other = lax.ppermute(own, "mp", g.core())
        return call(
            join_kernel,
            name,
            place,
            (CORES, IB),
            (own, other),
            [
                pl.BlockSpec((1, S, D), lambda k, i, place: (i * (1 - k) + (IB - 1) * k, 0, 0)),
                pl.BlockSpec((1, S, D), lambda k, i, place: (i * k, 0, 0)),
            ],
            shape((g.B, S, D), own.dtype),
            pl.BlockSpec((1, S, D), lambda k, i, place: ((place[0] ^ k) * IB + i, 0, 0)),
            [],
            0,
            2 * own.size * own.dtype.itemsize * 2,
        )

    input_grad = joined(grad_own_rows, "join_grad")
    output_own = call(
        functools.partial(output_kernel, g),
        "output",
        place,
        (IB,),
        (middle, params, *mixes),
        [row_spec, whole((8, D))] + [row_spec] * g.Y,
        shape((IB, S, D), BF),
        row_spec,
        [],
        0,
        8 << 20,
    )
    block_output = joined(output_own, "join_output")

    small = (mine.astype(F32) + lax.ppermute(theirs, "mp", g.core()).astype(F32)).astype(BF)
    small = tree(
        [small.astype(F32)]
        + [lax.ppermute(small, "dp", g.x(t)).astype(F32) for t in range(1, g.X)]
    ).astype(BF)
    pieces = [small] + [lax.ppermute(small, "dp", g.z(s)) for s in range(1, g.Z)]
    rows_shape = (g.HS + 16, D)
    small_dims = [
        (1, D),
        (1, D),
        (S, g.HS),
        (1, g.HS),
        (g.HS, S),
        (1, S),
        (1, D),
        (1, D),
        (1, g.FS),
        (1, D),
    ]
    smalls = call(
        functools.partial(small_kernel, g),
        "small",
        place,
        (1,),
        pieces,
        [whole(rows_shape)] * g.Z,
        [shape(d, F32) for d in small_dims],
        [whole(d) for d in small_dims],
        [],
        0,
        1 << 20,
    )
    smalls = [v if v.shape[0] > 1 else v[0] for v in smalls]

    half = g.FC // 2
    count = g.Z * g.X
    anywhere = pl.BlockSpec(memory_space=pl.ANY)
    act_list = [act_grid[s, t] for s in range(g.Z) for t in range(g.X)]
    group_own, group_give = call(
        functools.partial(group_kernel, g),
        "groups",
        place,
        (1,),
        (*act_list, *near, *far),
        [anywhere] * (len(act_list) + len(near) + len(far)),
        [shape((GROUPS, half, g.DX), F32), shape((GROUPS, half, g.DX), BF)],
        [whole((GROUPS, half, g.DX)), whole((GROUPS, half, g.DX))],
        [
            pltpu.VMEM((count, IB, S, g.FC), BF),
            pltpu.VMEM((count, IB, S + PAD, g.DX), BF),
            pltpu.VMEM((GROUPS, g.FC, g.DX), F32),
            pltpu.SemaphoreType.DMA((count,)),
            pltpu.SemaphoreType.DMA((len(near) + len(far),)),
        ],
        2 * count * IB * S * g.FC * g.DX,
        20 << 20,
    )
    group_other = lax.ppermute(group_give, "mp", g.core())
    one_group = pl.BlockSpec((1, half, g.DX), lambda k, place: (k, 0, 0))
    owned, scores = call(
        functools.partial(score_kernel, g),
        "scores",
        place,
        (GROUPS,),
        (group_own, group_other, query),
        [one_group, one_group, whole((g.Z, half, g.DC))],
        [shape((g.Z, half, g.DC), F32), shape((8, 128), F32)],
        [whole((g.Z, half, g.DC)), whole((8, 128))],
        [pltpu.VMEM((half, g.DX), F32)],
        0,
        8 << 20,
    )

    scores = scores + lax.ppermute(scores, "mp", g.core())
    scores = tree([scores] + [lax.ppermute(scores, "mp", g.y(u)) for u in range(1, g.Y)])
    scores = tree([scores] + [lax.ppermute(scores, "dp", g.x(t)) for t in range(1, g.X)])
    scores = tree([scores] + [lax.ppermute(scores, "dp", g.z(s)) for s in range(1, g.Z)])
    norm_raw = jnp.sqrt(scores[0, :GROUPS])
    average = jnp.mean(norm_raw)
    factor = average / jnp.maximum(norm_raw, average)
    influence = factor * scores[1, :GROUPS] / average
    group_norms = norm_raw / average

    back = [
        lax.ppermute(
            lax.dynamic_index_in_dim(owned, slot ^ r, 0, False),
            both,
            [(b, a) for a, b in g.owners(r)],
        )
        for r in range(g.Z)
    ]
    channel_reduce_gradient = jnp.concatenate(
        [select(back, (p % g.Z) ^ j) for j in range(g.Z)], axis=0
    )
    return (
        block_output,
        input_grad,
        *smalls[:8],
        channel_expand_gradient,
        smalls[8],
        channel_reduce_gradient,
        smalls[9],
        group_norms,
        influence,
    )


def solution(mesh):
    in_specs = (
        P("dp", None, None),
        P("dp", None),
        P("mp", "dp"),
        P(),
        P(),
        P(None, "mp"),
        P("mp"),
        P("mp", None),
        P(),
        P(),
        P(),
        P(None, "mp"),
        P("mp"),
        P("mp", None),
        P(),
        P("dp", None, None),
    )
    out_specs = (
        P("dp", None, None),
        P("dp", None, None),
        P(),
        P(),
        P(None, "mp"),
        P("mp"),
        P("mp", None),
        P(),
        P(),
        P(),
        P(None, "mp"),
        P("mp"),
        P("mp", "dp"),
        P(),
        P(),
        P(),
    )
    return jax.shard_map(
        per_device, mesh=mesh, in_specs=in_specs, out_specs=out_specs, check_vma=False
    )
```
